128 devices in a mesh: wave: 32 (over z, x_lo, y), lev: 4 (over x_hi, core).
Axes of the slice: x: 4 (x_hi: 2, x_lo: 2; x = x_hi * 2 + x_lo), y: 4, z: 4, core: 2. Of those that a mesh axis runs over, the one named last changes fastest.
Arguments:
- spectral: bfloat16 [2, 16, 640, 1281], P(None, 'lev', 'wave'), may hold values from -6 to 6
- legendre: bfloat16 [640, 1281, 256], P(('wave', 'lev')), may hold values from -0.0048828125 to 0.0048828125
- wave_table: int32 [640], replicated, may hold values from 0 to 639, each once
- courant_lon: float32 [16, 256, 5120], P('lev', 'wave'), may hold values from -0.35 to 0.35
- courant_lat: float32 [16, 256, 5120], P('lev', 'wave'), may hold values from -0.35 to 0.35
Outputs:
- tracer: float32 [16, 256, 5120], P('lev', 'wave')
The draws below stay inside these ranges and needn't reach their ends.
Inputs may be any that keep to these rules, and one draw needn't show every extreme that they name: A permutation of the pairs: slot s carries wavenumbers wave_table[s] and 1279 - wave_table[s].
All inputs are finite; a program needn't handle non-finite values.
Results may differ from the reference program's by a relative error of at most 0.003.
Values may be sent and summed in bfloat16 or wider, within the bound.
A program may use at most 64 MiB of HBM per device.

```python
import jax
import jax.numpy as jnp
from jax import lax

M = 1280
NLON = 5120
K = 1281
PAIRS = 640
LATW = 256
LEVELS = 16
PASSES = 4


def block_levels(key, dims, shards, least, top_value):
    level, own = 1.0, jax.random.fold_in(key, 6)
    for position, shards_of in shards:
        heights = jnp.exp(jax.random.uniform(jax.random.fold_in(own, position), (shards_of,), jnp.float32, least / len(shards), top_value / len(shards)))
        level = level * jnp.repeat(heights, dims[position] // shards_of).reshape([-1 if axis == position else 1 for axis in range(len(dims))])
    return level


def scatter_about(key, dims, deviation, limit, pieces=(), dtype=jnp.bfloat16):
    array = deviation * jax.random.normal(key, dims, jnp.float32)
    if pieces:
        array = array * block_levels(key, dims, pieces, -0.22, 0.18)
    return jnp.clip(array, -limit, limit).astype(dtype)


def setup_inputs(seed: int = 0) -> dict:
    splits = jax.random.split(jax.random.key(seed), 6)
    return {
        "spectral": scatter_about(splits[0], (2, LEVELS, PAIRS, K), 1.0, 6.0, ((1, 4), (2, 32))),
        "legendre": scatter_about(splits[1], (PAIRS, K, LATW), (K * M) ** -0.5, 0.0048828125, ((0, 128),)),
        "wave_table": jax.random.permutation(splits[2], PAIRS).astype(jnp.int32),
        "courant_lon": jnp.clip(jax.random.uniform(splits[3], (LEVELS, LATW, NLON), jnp.float32, -0.35, 0.35) * block_levels(splits[3], (LEVELS, LATW, NLON), ((0, 4), (1, 32)), -0.4, 0.0), -0.35, 0.35),
        "courant_lat": jnp.clip(jax.random.uniform(splits[4], (LEVELS, LATW, NLON), jnp.float32, -0.35, 0.35) * block_levels(splits[4], (LEVELS, LATW, NLON), ((0, 4), (1, 32)), -0.4, 0.0), -0.35, 0.35),
    }


def donor_flux(left_side, right_side, speed):
    return jnp.maximum(speed, 0.0) * left_side + jnp.minimum(speed, 0.0) * right_side


def from_west(field):
    return jnp.roll(field, 1, axis=-1)


def from_east(field):
    return jnp.roll(field, -1, axis=-1)


def floored_ratio(numerator, denominator):
    return numerator / jnp.maximum(denominator, 1.0)


def mpdata_pass(tracer_rows, speed_lon, speed_lat, inside):
    flux_lon = donor_flux(from_west(tracer_rows), tracer_rows, speed_lon)
    flux_lat = donor_flux(tracer_rows[..., :-1, :], tracer_rows[..., 1:, :], speed_lat[..., 1:, :])
    upwind = tracer_rows[..., 1:-1, :] - (from_east(flux_lon) - flux_lon)[..., 1:-1, :] - (flux_lat[..., 1:, :] - flux_lat[..., :-1, :])
    upwind = jnp.where(inside[1:-1, None], upwind, 0.0)
    west_side = from_west(upwind)
    centre = upwind[..., 1:-1, :]
    left_cell = west_side[..., 1:-1, :]
    upper_row = upwind[..., 2:, :]
    upper_west = west_side[..., 2:, :]
    lower_row = upwind[..., :-2, :]
    lower_west = west_side[..., :-2, :]
    grad_lon = floored_ratio(centre - left_cell, jnp.abs(centre) + jnp.abs(left_cell))
    cross_lon = 0.5 * floored_ratio(upper_row + upper_west - lower_row - lower_west, jnp.abs(upper_row) + jnp.abs(upper_west) + jnp.abs(lower_row) + jnp.abs(lower_west))
    speed_x = speed_lon[..., 2:-2, :]
    lat_west = from_west(speed_lat)
    mean_lat = 0.25 * (speed_lat[..., 2:-2, :] + speed_lat[..., 3:-1, :] + lat_west[..., 2:-2, :] + lat_west[..., 3:-1, :])
    anti_lon = (jnp.abs(speed_x) - speed_x * speed_x) * grad_lon - speed_x * mean_lat * cross_lon
    above_row = upwind[..., 1:, :]
    below_row = upwind[..., :-1, :]
    grad_lat = floored_ratio(above_row - below_row, jnp.abs(above_row) + jnp.abs(below_row))
    above_east = from_east(above_row)
    below_east = from_east(below_row)
    above_west = from_west(above_row)
    below_west = from_west(below_row)
    cross_lat = 0.5 * floored_ratio(above_east + below_east - above_west - below_west, jnp.abs(above_east) + jnp.abs(below_east) + jnp.abs(above_west) + jnp.abs(below_west))
    speed_y = speed_lat[..., 2:-1, :]
    lon_east = from_east(speed_lon)
    mean_lon = 0.25 * (speed_lon[..., 2:-1, :] + lon_east[..., 2:-1, :] + speed_lon[..., 1:-2, :] + lon_east[..., 1:-2, :])
    anti_lat = (jnp.abs(speed_y) - speed_y * speed_y) * grad_lat - speed_y * mean_lon * cross_lat
    corr_lon = donor_flux(left_cell, centre, anti_lon)
    corr_lat = donor_flux(below_row, above_row, anti_lat)
    second = centre - (from_east(corr_lon) - corr_lon) - (corr_lat[..., 1:, :] - corr_lat[..., :-1, :])
    return jnp.where(inside[2:-2, None], second, 0.0)


def reference(spectral, legendre, wave_table, courant_lon, courant_lat):
    def one_slot(slot_items):
        spectra, table_rows, pair_id = slot_items
        lower_part = jnp.arange(K) < M - pair_id
        nothing = jnp.zeros((), jnp.bfloat16)
        halves = jnp.stack([jnp.where(lower_part, spectra, nothing), jnp.where(lower_part, nothing, spectra)], 0)
        return jnp.einsum("wrlk,kt->wrlt", halves.astype(jnp.float32), table_rows.astype(jnp.float32), precision=lax.Precision.HIGHEST)

    by_slot = jnp.transpose(spectral, (2, 0, 1, 3))
    terms = lax.map(one_slot, (by_slot, legendre, wave_table))
    coefficients = lax.optimization_barrier(terms.astype(jnp.bfloat16)).astype(jnp.float32)
    numbers = jnp.stack([wave_table, M - 1 - wave_table], 1).reshape(-1).astype(jnp.int32)
    placed = jnp.zeros((M, 2, LEVELS, LATW), jnp.float32).at[numbers].set(coefficients.reshape(M, 2, LEVELS, LATW))
    real_part = jnp.transpose(placed[:, 0], (1, 2, 0))
    imag_part = jnp.transpose(placed[:, 1], (1, 2, 0))
    spectrum = lax.complex(real_part, imag_part)
    spectrum = jnp.pad(spectrum, ((0, 0), (0, 0), (0, NLON // 2 + 1 - M)))
    grid = (jnp.fft.irfft(spectrum, n=NLON, axis=-1) * NLON).astype(jnp.float32)

    def advect(level_items):
        field, speed_lon, speed_lat = level_items
        row_index = jnp.arange(-2, LATW + 2)
        inside = (row_index >= 0) & (row_index < LATW)
        padded_lon = jnp.pad(speed_lon, ((2, 2), (0, 0)))
        padded_lat = jnp.pad(speed_lat, ((2, 2), (0, 0)))
        for number in range(PASSES):
            field = mpdata_pass(jnp.pad(field, ((2, 2), (0, 0))), padded_lon, padded_lat, inside)
        return field

    return lax.map(advect, (grid, courant_lon, courant_lat))
```

```python
import math

import jax
import jax.numpy as jnp
import numpy as np
from jax import lax
from jax.experimental import pallas as pl
from jax.experimental.pallas import tpu as pltpu
from jax.sharding import PartitionSpec as P

M = 1280
NLON = 5120
K = 1281
PASSES = 4
WAVES = 32
LEVS = 4
SLOTS = 5
ROWS = 8
NF = 40
NB = 128
F32 = jnp.float32
BF16 = jnp.bfloat16
MESH = pl.DeviceIdType.MESH


def split_table(values):
    high = values.astype(np.float32).astype(BF16)
    low = (values - high.astype(np.float64)).astype(np.float32).astype(BF16)
    return high, low


def first_stage_tables():
    g = np.arange(5)[:, None, None, None]
    h = np.arange(2)[None, :, None, None]
    f8 = np.arange(8)[None, None, :, None]
    p1 = np.arange(16)[None, None, None, :]
    m = np.where(h == 0, 40 * p1 + 8 * g + f8, M - 1 - (40 * p1 + 8 * (4 - g) + f8))
    m = m.reshape(5, 256, 1)
    angle = 2.0 * math.pi / NLON * ((m * np.arange(NB)[None, None, :]) % NLON)
    weight = np.where(m == 0, 1.0, 2.0)
    return split_table(np.concatenate([weight * np.cos(angle), weight * np.sin(angle)], -1))


def second_stage_table():
    row = np.arange(NF)
    place = 5 * (row % 8) + row // 8
    angle = 2.0 * math.pi / NF * ((place[:, None] * np.arange(NF)[None, :]) % NF)
    high, low = split_table(np.concatenate([np.cos(angle), -np.sin(angle)], -1))
    return np.concatenate([high, low, high], -1)


def pack_table():
    t8 = np.arange(8)[:, None, None]
    lane = np.arange(128)[None, :, None]
    h, v, c, l = lane // 32, lane // 8 % 4, lane // 4 % 2, lane % 4
    goal = v * 128 + h * 64 + c * 32 + t8 * 4 + l
    hit = (goal == np.arange(512)[None, None, :]) & (lane < 64)
    return hit.astype(np.float32).astype(BF16)


def dot(a, b):
    return jnp.dot(a, b, preferred_element_type=F32)


def legendre_kernel(pairs_ref, x_ref, leg_ref, pack_ref, msg_ref, turned, lined):
    lined[...] = jnp.zeros_like(lined)
    lane = lax.broadcasted_iota(jnp.int32, (1, K), 1)
    for s in range(SLOTS):
        low = lane < (M - pairs_ref[s])
        spectra = x_ref[:, s].reshape(32, K)
        zero = jnp.zeros_like(spectra)
        halves = jnp.concatenate(
            [jnp.where(low, spectra, zero), jnp.where(low, zero, spectra)], 0
        )
        total = dot(halves[:, : K - 1], leg_ref[s, : K - 1, :])
        last = spectra[:, K - 1 : K].astype(F32) * leg_ref[s, K - 1 : K, :].astype(F32)
        total = jnp.concatenate([total[:32], total[32:] + last], 0)
        rounded = total.astype(BF16).astype(F32)
        square = jnp.concatenate([rounded, jnp.zeros_like(rounded)], 0)
        turned[...] = square.T
        for t8 in range(8):
            lined[t8, pl.ds(s, WAVES, stride=8), :] = turned[pl.ds(t8, WAVES, stride=8), :]
    total = dot(lined[0].astype(BF16), pack_ref[0])
    for t8 in range(1, 8):
        total += dot(lined[t8].astype(BF16), pack_ref[t8])
    packed = total.astype(BF16)
    for v in range(LEVS):
        msg_ref[:, v] = packed[:, v * 128 : (v + 1) * 128].reshape(WAVES, 8, 128)


def west(v, edge):
    r = pltpu.roll(v, 1, 1)
    before = jnp.concatenate([pltpu.roll(r[32:40], 1, 0), r[0:32]], 0)
    return jnp.where(edge, before, r)


def east(v, edge):
    r = pltpu.roll(v, 127, 1)
    after = jnp.concatenate([r[8:40], pltpu.roll(r[0:8], 7, 0)], 0)
    return jnp.where(edge, after, r)


def ratio(x, y):
    return x / jnp.maximum(y, 1.0)


def advance_kernel(
    tbl_ref, recv_ref, hi_ref, lo_ref, two_ref, lon_ref, lat_ref, out_ref,
    qt, ast, fld, cx, cy, cxp, cxm, cyp, cym, ax, bx, ay, by,
    q1s, wst, swe, awe, dew, aew, gys, stage, halo,
    csend, crecv, hsend, hrecv,
):
    me = lax.axis_index("wave")
    up = lax.rem(me + 1, WAVES)
    down = lax.rem(me + WAVES - 1, WAVES)
    has_up = me < WAVES - 1
    has_down = me > 0

    barrier = pltpu.get_barrier_semaphore()
    for nb in (up, down):
        pl.semaphore_signal(barrier, inc=1, device_id={"wave": nb}, device_id_type=MESH)
    pl.semaphore_wait(barrier, 2)

    def remote(src, dst, ssem, rsem, nb):
        return pltpu.make_async_remote_copy(
            src_ref=src, dst_ref=dst, send_sem=ssem, recv_sem=rsem,
            device_id={"wave": nb}, device_id_type=MESH,
        )

    def repack(l, carry):
        for i in range(ROWS):
            for k in range(5):
                cx[i + 1, l, 8 * k : 8 * k + 8, :] = lon_ref[l, pl.ds(8 * k + i, 8, stride=40), :]
                cy[i + 1, l, 8 * k : 8 * k + 8, :] = lat_ref[l, pl.ds(8 * k + i, 8, stride=40), :]
        return carry

    lax.fori_loop(0, LEVS, repack, 0)
    courant = [
        remote(cx.at[8], cx.at[0], csend.at[0], crecv.at[0], up),
        remote(cy.at[8], cy.at[0], csend.at[1], crecv.at[1], up),
        remote(cx.at[1], cx.at[9], csend.at[2], crecv.at[2], down),
        remote(cy.at[pl.ds(1, 2)], cy.at[pl.ds(9, 2)], csend.at[3], crecv.at[3], down),
    ]
    for c in courant:
        c.start()

    row = lax.broadcasted_iota(jnp.int32, (640, 1), 0)
    pair_of = 40 * (row % 16) + 8 * (row // 128) + row // 16 % 8
    choose = jnp.where(tbl_ref[...] == pair_of, 1.0, 0.0).astype(BF16)
    ordered = dot(choose, recv_ref[...])
    for g in range(5):
        qt[g] = ordered[g * 128 : (g + 1) * 128, :].T

    lane = lax.broadcasted_iota(jnp.int32, (8, 128), 1)
    sub = lax.broadcasted_iota(jnp.int32, (8, 128), 0)
    masks = (lane // 16 == sub, lane // 16 == 7 - sub)

    def first(g, carry):
        total = None
        for h in range(2):
            source = g if h == 0 else 4 - g
            rows = slice(h * 128, h * 128 + 128)
            th, tl = hi_ref[g, rows, :], lo_ref[g, rows, :]
            for c in range(2):
                blocks = []
                for x in range(32):
                    line = qt[source, pl.ds(h * 64 + c * 32 + x, 8, stride=0), :]
                    blocks.append(jnp.where(masks[h], line, 0.0))
                lhs = jnp.concatenate(blocks, 0).astype(BF16)
                for table in (th, tl):
                    if c == 1:
                        table = jnp.concatenate([-table[:, 128:], table[:, :128]], 1)
                    term = dot(lhs, table)
                    total = term if total is None else total + term
        total = total.reshape(32, 8, 256)
        at = pl.multiple_of(8 * g, 8)
        ast[:, 0, pl.ds(at, 8), :] = total[:, :, :128]
        ast[:, 1, pl.ds(at, 8), :] = total[:, :, 128:]
        return carry

    lax.fori_loop(0, 5, first, 0)

    def halo_copies(parity, l):
        return [
            remote(stage.at[parity, 1, l], halo.at[parity, 0, l],
                   hsend.at[parity, 0, l], hrecv.at[parity, 0, l], up),
            remote(stage.at[parity, 0, l], halo.at[parity, 1, l],
                   hsend.at[parity, 1, l], hrecv.at[parity, 1, l], down),
        ]

    def send_halo(parity, l):
        for i in range(2):
            stage[parity, 0, l, i] = fld[2 + i, l].astype(BF16)
            stage[parity, 1, l, i] = fld[8 + i, l].astype(BF16)
        for c in halo_copies(parity, l):
            c.start()

    def second(l, carry):
        for t in range(0, ROWS, 2):
            parts = []
            for u in (t, t + 1):
                both = ast[u * 4 + l].reshape(80, 128)
                high = both.astype(BF16)
                low = (both - high.astype(F32)).astype(BF16)
                parts.append(jnp.concatenate([high, high, low], 0))
            values = dot(two_ref[...], jnp.concatenate(parts, 1))
            fld[2 + t, l] = values[:, :128]
            fld[3 + t, l] = values[:, 128:]
        send_halo(0, l)
        return carry

    lax.fori_loop(0, LEVS, second, 0)

    for c in courant:
        c.wait()
    lanes = lax.broadcasted_iota(jnp.int32, (NF, 128), 1)
    first_lane = lanes == 0
    last_lane = lanes == 127

    def terms(l, carry):
        zero = jnp.zeros((NF, 128), F32)
        cx[0, l] = jnp.where(has_down, cx[0, l], zero)
        cy[0, l] = jnp.where(has_down, cy[0, l], zero)
        cx[9, l] = jnp.where(has_up, cx[9, l], zero)
        cy[9, l] = jnp.where(has_up, cy[9, l], zero)
        cy[10, l] = jnp.where(has_up, cy[10, l], zero)
        for r in range(11):
            v = cy[r, l]
            cyp[r, l] = jnp.maximum(v, 0.0)
            cym[r, l] = jnp.minimum(v, 0.0)
            if r < 10:
                u = cx[r, l]
                cxp[r, l] = jnp.maximum(u, 0.0)
                cxm[r, l] = jnp.minimum(u, 0.0)
        for i in range(ROWS):
            u = cx[i + 1, l]
            ax[i, l] = jnp.abs(u) - u * u
            pair = cy[i + 1, l] + cy[i + 2, l]
            bx[i, l] = (u * 0.125) * (pair + west(pair, first_lane))
        for i in range(ROWS + 1):
            v = cy[i + 1, l]
            ay[i, l] = jnp.abs(v) - v * v
            pair = cx[i + 1, l] + cx[i, l]
            by[i, l] = (v * 0.125) * (pair + east(pair, last_lane))
        return carry

    lax.fori_loop(0, LEVS, terms, 0)

    def level_pass(step, carry):
        number = step // LEVS
        l = step % LEVS
        parity = number % 2
        for c in halo_copies(parity, l):
            c.wait()
        zero = jnp.zeros((NF, 128), F32)
        for i in range(2):
            fld[i, l] = jnp.where(has_down, halo[parity, 0, l, i].astype(F32), zero)
            fld[10 + i, l] = jnp.where(has_up, halo[parity, 1, l, i].astype(F32), zero)
        flux = None
        for r in range(-1, 9):
            q = fld[r + 2, l]
            if flux is None:
                flux = cyp[r + 1, l] * fld[r + 1, l] + cym[r + 1, l] * q
            above = cyp[r + 2, l] * q + cym[r + 2, l] * fld[r + 3, l]
            fx = cxp[r + 1, l] * west(q, first_lane) + cxm[r + 1, l] * q
            v = q - (east(fx, last_lane) - fx) - (above - flux)
            flux = above
            if r == -1:
                v = jnp.where(has_down, v, zero)
            if r == 8:
                v = jnp.where(has_up, v, zero)
            w = west(v, first_lane)
            e = east(v, last_lane)
            aw = jnp.abs(w)
            q1s[r + 1] = v
            wst[r + 1] = w
            swe[r + 1] = v + w
            awe[r + 1] = jnp.abs(v) + aw
            dew[r + 1] = e - w
            aew[r + 1] = jnp.abs(e) + aw

        def face(i):
            a, b = q1s[i + 1], q1s[i]
            grad = ratio(a - b, jnp.abs(a) + jnp.abs(b))
            cross = ratio(dew[i + 1] + dew[i], aew[i + 1] + aew[i])
            vy = ay[i, l] * grad - by[i, l] * cross
            gys[i] = jnp.maximum(vy, 0.0) * b + jnp.minimum(vy, 0.0) * a

        def finish(i):
            v, w = q1s[i + 1], wst[i + 1]
            grad = ratio(v - w, awe[i + 1])
            cross = ratio(swe[i + 2] - swe[i], awe[i + 2] + awe[i])
            vx = ax[i, l] * grad - bx[i, l] * cross
            gx = jnp.maximum(vx, 0.0) * w + jnp.minimum(vx, 0.0) * v
            fld[i + 2, l] = v - (east(gx, last_lane) - gx) - (gys[i + 1] - gys[i])

        for i in (0, 1, 2):
            face(i)
        for i in (0, 1):
            finish(i)
        for i in (6, 7, 8):
            face(i)
        for i in (6, 7):
            finish(i)

        @pl.when(number < PASSES - 1)
        def _():
            send_halo(1 - parity, l)

        for i in (3, 4, 5):
            face(i)
        for i in (2, 3, 4, 5):
            finish(i)
        return carry

    lax.fori_loop(0, PASSES * LEVS, level_pass, 0)

    def deliver(l, carry):
        for i in range(ROWS):
            for k in range(5):
                out_ref[l, pl.ds(8 * k + i, 8, stride=40), :] = fld[i + 2, l, 8 * k : 8 * k + 8, :]
        return carry

    lax.fori_loop(0, LEVS, deliver, 0)


def tiles_of(winds):
    return winds.reshape(LEVS, ROWS, NF, NB).transpose(0, 2, 1, 3).reshape(LEVS, NF * ROWS, NB)


def body(spectral, legendre, wave_table, courant_lon, courant_lat):
    wave_rank = lax.axis_index("wave")
    level_rank = lax.axis_index("lev")
    own_pairs = lax.dynamic_slice_in_dim(
        wave_table, (wave_rank * LEVS + level_rank) * SLOTS, SLOTS
    )
    table = jnp.pad(wave_table.reshape(128, SLOTS), ((0, 0), (0, 3)), constant_values=-1)
    table = table.reshape(1, 1024)
    parts = spectral.reshape(2, 4, LEVS, SLOTS, K).transpose(2, 3, 0, 1, 4)
    parts = parts.reshape(LEVS, SLOTS, 8, K)
    arrived = lax.all_to_all(parts, "lev", split_axis=0, concat_axis=0, tiled=True)

    vmem = pl.BlockSpec(memory_space=pltpu.VMEM)
    smem = pl.BlockSpec(memory_space=pltpu.SMEM)
    messages = pl.pallas_call(
        legendre_kernel,
        out_shape=jax.ShapeDtypeStruct((WAVES, LEVS, 8, 128), BF16),
        in_specs=[smem, vmem, vmem, vmem],
        out_specs=vmem,
        scratch_shapes=[
            pltpu.VMEM((256, 128), F32),
            pltpu.VMEM((8, 256, 128), F32),
        ],
        name="legendre",
    )(own_pairs, arrived, legendre, jnp.asarray(pack_table()))
    received = lax.all_to_all(
        messages.reshape(128, 8, 128), ("wave", "lev"), split_axis=0, concat_axis=0, tiled=True
    )
    high, low = first_stage_tables()
    big = lambda rows: pltpu.VMEM((rows, LEVS, NF, NB), F32)
    small = lambda rows: pltpu.VMEM((rows, NF, NB), F32)
    out = pl.pallas_call(
        advance_kernel,
        out_shape=jax.ShapeDtypeStruct((LEVS, NF * ROWS, NB), F32),
        in_specs=[vmem] * 7,
        out_specs=vmem,
        scratch_shapes=[
            pltpu.VMEM((5, 128, 128), F32),
            pltpu.VMEM((32, 2, NF, NB), F32),
            big(12), big(10), big(11), big(10), big(10), big(11), big(11),
            big(8), big(8), big(9), big(9),
            small(10), small(10), small(10), small(10), small(10), small(10), small(9),
            pltpu.VMEM((2, 2, LEVS, 2, NF, NB), BF16),
            pltpu.VMEM((2, 2, LEVS, 2, NF, NB), BF16),
            pltpu.SemaphoreType.DMA((4,)),
            pltpu.SemaphoreType.DMA((4,)),
            pltpu.SemaphoreType.DMA((2, 2, LEVS)),
            pltpu.SemaphoreType.DMA((2, 2, LEVS)),
        ],
        compiler_params=pltpu.CompilerParams(collective_id=0, has_side_effects=True),
        name="advance",
    )(
        table, received.reshape(1024, 128), jnp.asarray(high), jnp.asarray(low),
        jnp.asarray(second_stage_table()), tiles_of(courant_lon), tiles_of(courant_lat),
    )
    out = out.reshape(LEVS, NF, ROWS, NB).transpose(0, 2, 1, 3)
    return out.reshape(LEVS, ROWS, NLON)


def solution(mesh):
    placed = (
        P(None, "lev", "wave", None),
        P(("wave", "lev"), None, None),
        P(),
        P("lev", "wave", None),
        P("lev", "wave", None),
    )
    return jax.shard_map(
        body, mesh=mesh, in_specs=placed, out_specs=P("lev", "wave", None), check_vma=False
    )
```

```python
import math

import jax
import jax.numpy as jnp
import numpy as np
from jax import lax
from jax.experimental import pallas as pl
from jax.experimental.pallas import tpu as pltpu
from jax.sharding import PartitionSpec as P

M = 1280
NLON = 5120
K = 1281
PASSES = 4
WAVES = 32
LEVS = 4
SLOTS = 5
ROWS = 8
NF = 40
NB = 128
F32 = jnp.float32
BF16 = jnp.bfloat16
MESH = pl.DeviceIdType.MESH


def split_table(values):
    high = values.astype(np.float32).astype(BF16)
    low = (values - high.astype(np.float64)).astype(np.float32).astype(BF16)
    return high, low


def first_stage_tables():
    g = np.arange(5)[:, None, None, None]
    h = np.arange(2)[None, :, None, None]
    f8 = np.arange(8)[None, None, :, None]
    p1 = np.arange(16)[None, None, None, :]
    m = np.where(h == 0, 40 * p1 + 8 * g + f8, M - 1 - (40 * p1 + 8 * (4 - g) + f8))
    m = m.reshape(5, 256, 1)
    angle = 2.0 * math.pi / NLON * ((m * np.arange(NB)[None, None, :]) % NLON)
    weight = np.where(m == 0, 1.0, 2.0)
    return split_table(np.concatenate([weight * np.cos(angle), weight * np.sin(angle)], -1))


def second_stage_table():
    row = np.arange(NF)
    place = 5 * (row % 8) + row // 8
    angle = 2.0 * math.pi / NF * ((place[:, None] * np.arange(NF)[None, :]) % NF)
    high, low = split_table(np.concatenate([np.cos(angle), -np.sin(angle)], -1))
    return np.concatenate([high, low, high], -1)


def pack_table():
    t8 = np.arange(8)[:, None, None]
    lane = np.arange(128)[None, :, None]
    h, v, c, l = lane // 32, lane // 8 % 4, lane // 4 % 2, lane % 4
    goal = v * 128 + h * 64 + c * 32 + t8 * 4 + l
    hit = (goal == np.arange(512)[None, None, :]) & (lane < 64)
    return hit.astype(np.float32).astype(BF16)


def dot(a, b):
    return jnp.dot(a, b, preferred_element_type=F32)


def west(v, edge):
    r = pltpu.roll(v, 1, 1)
    before = jnp.concatenate([pltpu.roll(r[32:40], 1, 0), r[0:32]], 0)
    return jnp.where(edge, before, r)


def east(v, edge):
    r = pltpu.roll(v, 127, 1)
    after = jnp.concatenate([r[8:40], pltpu.roll(r[0:8], 7, 0)], 0)
    return jnp.where(edge, after, r)


def ratio(x, y):
    return x / jnp.maximum(y, 1.0)


def whole_kernel(
    pairs_ref, tbl_ref, spec_hbm, leg_hbm, lon_hbm, lat_hbm, pack_hbm, hi_hbm, lo_hbm, two_hbm,
    out_ref,
    leg_ref, lon_ref, lat_ref, pack_ref, hi_ref, lo_ref, two_ref,
    arrived, turned, lined, msgs, recv, choose,
    qt, ast, fld, cx, cy, cxp, cxm, cyp, cym, ax, bx, ay, by,
    q1s, wst, swe, awe, dew, aew, gys, stage, halo,
    lsem, ssend, srecv, asend, arecv, csend, crecv, hsend, hrecv,
):
    me = lax.axis_index("wave")
    lev = lax.axis_index("lev")
    rank = me * LEVS + lev
    up = lax.rem(me + 1, WAVES)
    down = lax.rem(me + WAVES - 1, WAVES)
    has_up = me < WAVES - 1
    has_down = me > 0

    barrier = pltpu.get_barrier_semaphore()

    def greet(step, carry):
        peer = lax.rem(rank + step, 128)
        pl.semaphore_signal(
            barrier, inc=1, device_id={"wave": peer // LEVS, "lev": peer % LEVS},
            device_id_type=MESH,
        )
        return carry

    lax.fori_loop(1, 128, greet, 0)

    local = [
        pltpu.make_async_copy(a, b, lsem.at[n])
        for n, (a, b) in enumerate(
            [(lon_hbm, lon_ref), (lat_hbm, lat_ref), (leg_hbm, leg_ref), (pack_hbm, pack_ref),
             (hi_hbm, hi_ref), (lo_hbm, lo_ref), (two_hbm, two_ref)]
        )
    ]
    own = pltpu.make_async_copy(
        spec_hbm.at[pl.ds(lev * SLOTS, SLOTS)], arrived.at[lev], lsem.at[7]
    )
    for copy in local:
        copy.start()
    own.start()

    def remote(src, dst, ssem, rsem, nb):
        return pltpu.make_async_remote_copy(
            src_ref=src, dst_ref=dst, send_sem=ssem, recv_sem=rsem,
            device_id={"wave": nb}, device_id_type=MESH,
        )

    local[0].wait()
    local[1].wait()

    def repack(l, carry):
        for i in range(ROWS):
            for k in range(5):
                cx[i + 1, l, 8 * k : 8 * k + 8, :] = lon_ref[l, pl.ds(8 * k + i, 8, stride=40), :]
                cy[i + 1, l, 8 * k : 8 * k + 8, :] = lat_ref[l, pl.ds(8 * k + i, 8, stride=40), :]
        return carry


    lax.fori_loop(0, LEVS, repack, 0)

    row = lax.broadcasted_iota(jnp.int32, (640, 1), 0)
    pair_of = 40 * (row % 16) + 8 * (row // 128) + row // 16 % 8
    choose[...] = jnp.where(tbl_ref[...] == pair_of, 1.0, 0.0).astype(BF16)
    lined[...] = jnp.zeros_like(lined)

    pl.semaphore_wait(barrier, 127)

    def spectral_copy(step, s):
        peer = lax.rem(lev + step, LEVS)
        return pltpu.make_async_remote_copy(
            src_ref=spec_hbm.at[peer * SLOTS + s],
            dst_ref=arrived.at[lev, s],
            send_sem=ssend.at[step - 1, s],
            recv_sem=srecv.at[step - 1, s],
            device_id={"lev": peer},
            device_id_type=MESH,
        )

    for s in range(SLOTS):
        for step in range(1, LEVS):
            spectral_copy(step, s).start()
    courant = [
        remote(cx.at[8], cx.at[0], csend.at[0], crecv.at[0], up),
        remote(cy.at[8], cy.at[0], csend.at[1], crecv.at[1], up),
        remote(cx.at[1], cx.at[9], csend.at[2], crecv.at[2], down),
        remote(cy.at[pl.ds(1, 2)], cy.at[pl.ds(9, 2)], csend.at[3], crecv.at[3], down),
    ]
    for copy in courant:
        copy.start()
    for copy in local[2:]:
        copy.wait()
    own.wait()

    klane = lax.broadcasted_iota(jnp.int32, (1, K), 1)

    def legendre_slot(s, carry):
        for step in range(1, LEVS):
            spectral_copy(step, s).wait()
        low = klane < (M - pairs_ref[rank * SLOTS + s])
        spectra = arrived[:, s].reshape(32, K)
        zero = jnp.zeros_like(spectra)
        halves = jnp.concatenate(
            [jnp.where(low, spectra, zero), jnp.where(low, zero, spectra)], 0
        )
        total = dot(halves[:, : K - 1], leg_ref[s, : K - 1, :])
        last = spectra[:, K - 1 : K].astype(F32) * leg_ref[s, K - 1 : K, :].astype(F32)
        total = jnp.concatenate([total[:32], total[32:] + last], 0)
        rounded = total.astype(BF16).astype(F32)
        square = jnp.concatenate([rounded, jnp.zeros_like(rounded)], 0)
        turned[...] = square.T
        for t8 in range(8):
            lined[t8, pl.ds(s, WAVES, stride=8), :] = turned[pl.ds(t8, WAVES, stride=8), :]
        return carry

    for s in range(SLOTS):
        legendre_slot(s, 0)
    total = dot(lined[0].astype(BF16), pack_ref[0])
    for t8 in range(1, 8):
        total += dot(lined[t8].astype(BF16), pack_ref[t8])
    packed = total.astype(BF16)
    for v in range(LEVS):
        msgs[:, v] = packed[:, v * 128 : (v + 1) * 128].reshape(WAVES, 8, 128)

    recv[rank] = msgs[me, lev]

    def scatter(step, carry):
        peer = lax.rem(rank + step, 128)
        pw, pv = peer // LEVS, peer % LEVS
        pltpu.make_async_remote_copy(
            src_ref=msgs.at[pw, pv], dst_ref=recv.at[rank], send_sem=asend, recv_sem=arecv,
            device_id={"wave": pw, "lev": pv}, device_id_type=MESH,
        ).start()
        return carry

    lax.fori_loop(1, 128, scatter, 0)

    for copy in courant:
        copy.wait()
    lanes = lax.broadcasted_iota(jnp.int32, (NF, 128), 1)
    first_lane = lanes == 0
    last_lane = lanes == 127

    def terms(l, carry):
        zero = jnp.zeros((NF, 128), F32)
        cx[0, l] = jnp.where(has_down, cx[0, l], zero)
        cy[0, l] = jnp.where(has_down, cy[0, l], zero)
        cx[9, l] = jnp.where(has_up, cx[9, l], zero)
        cy[9, l] = jnp.where(has_up, cy[9, l], zero)
        cy[10, l] = jnp.where(has_up, cy[10, l], zero)
        for r in range(11):
            v = cy[r, l]
            cyp[r, l] = jnp.maximum(v, 0.0)
            cym[r, l] = jnp.minimum(v, 0.0)
            if r < 10:
                u = cx[r, l]
                cxp[r, l] = jnp.maximum(u, 0.0)
                cxm[r, l] = jnp.minimum(u, 0.0)
        for i in range(ROWS):
            u = cx[i + 1, l]
            ax[i, l] = jnp.abs(u) - u * u
            pair = cy[i + 1, l] + cy[i + 2, l]
            bx[i, l] = (u * 0.125) * (pair + west(pair, first_lane))
        for i in range(ROWS + 1):
            v = cy[i + 1, l]
            ay[i, l] = jnp.abs(v) - v * v
            pair = cx[i + 1, l] + cx[i, l]
            by[i, l] = (v * 0.125) * (pair + east(pair, last_lane))
        return carry


    lax.fori_loop(0, LEVS, terms, 0)

    blocks127 = recv.at[pl.ds(0, 127)]
    pltpu.make_async_copy(blocks127, blocks127, arecv).wait()
    pltpu.make_async_copy(blocks127, blocks127, asend).wait()

    ordered = dot(choose[...], recv[...].reshape(1024, 128))
    for g in range(5):
        qt[g] = ordered[g * 128 : (g + 1) * 128, :].T

    lane = lax.broadcasted_iota(jnp.int32, (8, 128), 1)
    sub = lax.broadcasted_iota(jnp.int32, (8, 128), 0)
    masks = (lane // 16 == sub, lane // 16 == 7 - sub)

    def first(g, carry):
        total = None
        for h in range(2):
            source = g if h == 0 else 4 - g
            rows = slice(h * 128, h * 128 + 128)
            th, tl = hi_ref[g, rows, :], lo_ref[g, rows, :]
            for c in range(2):
                blocks = []
                for x in range(32):
                    line = qt[source, pl.ds(h * 64 + c * 32 + x, 8, stride=0), :]
                    blocks.append(jnp.where(masks[h], line, 0.0))
                lhs = jnp.concatenate(blocks, 0).astype(BF16)
                for table in (th, tl):
                    if c == 1:
                        table = jnp.concatenate([-table[:, 128:], table[:, :128]], 1)
                    term = dot(lhs, table)
                    total = term if total is None else total + term
        total = total.reshape(32, 8, 256)
        at = pl.multiple_of(8 * g, 8)
        ast[:, 0, pl.ds(at, 8), :] = total[:, :, :128]
        ast[:, 1, pl.ds(at, 8), :] = total[:, :, 128:]
        return carry

    lax.fori_loop(0, 5, first, 0)

    def halo_copies(parity, l):
        return [
            remote(stage.at[parity, 1, l], halo.at[parity, 0, l],
                   hsend.at[parity, 0, l], hrecv.at[parity, 0, l], up),
            remote(stage.at[parity, 0, l], halo.at[parity, 1, l],
                   hsend.at[parity, 1, l], hrecv.at[parity, 1, l], down),
        ]

    def send_halo(parity, l):
        for i in range(2):
            stage[parity, 0, l, i] = fld[2 + i, l].astype(BF16)
            stage[parity, 1, l, i] = fld[8 + i, l].astype(BF16)
        for c in halo_copies(parity, l):
            c.start()

    def second(l, carry):
        for t in range(0, ROWS, 2):
            parts = []
            for u in (t, t + 1):
                both = ast[u * 4 + l].reshape(80, 128)
                high = both.astype(BF16)
                low = (both - high.astype(F32)).astype(BF16)
                parts.append(jnp.concatenate([high, high, low], 0))
            values = dot(two_ref[...], jnp.concatenate(parts, 1))
            fld[2 + t, l] = values[:, :128]
            fld[3 + t, l] = values[:, 128:]
        send_halo(0, l)
        return carry

    lax.fori_loop(0, LEVS, second, 0)

    def level_pass(step, carry):
        number = step // LEVS
        l = step % LEVS
        parity = number % 2
        for c in halo_copies(parity, l):
            c.wait()
        zero = jnp.zeros((NF, 128), F32)
        for i in range(2):
            fld[i, l] = jnp.where(has_down, halo[parity, 0, l, i].astype(F32), zero)
            fld[10 + i, l] = jnp.where(has_up, halo[parity, 1, l, i].astype(F32), zero)
        flux = None
        for r in range(-1, 9):
            q = fld[r + 2, l]
            if flux is None:
                flux = cyp[r + 1, l] * fld[r + 1, l] + cym[r + 1, l] * q
            above = cyp[r + 2, l] * q + cym[r + 2, l] * fld[r + 3, l]
            fx = cxp[r + 1, l] * west(q, first_lane) + cxm[r + 1, l] * q
            v = q - (east(fx, last_lane) - fx) - (above - flux)
            flux = above
            if r == -1:
                v = jnp.where(has_down, v, zero)
            if r == 8:
                v = jnp.where(has_up, v, zero)
            w = west(v, first_lane)
            e = east(v, last_lane)
            aw = jnp.abs(w)
            q1s[r + 1] = v
            wst[r + 1] = w
            swe[r + 1] = v + w
            awe[r + 1] = jnp.abs(v) + aw
            dew[r + 1] = e - w
            aew[r + 1] = jnp.abs(e) + aw

        def face(i):
            a, b = q1s[i + 1], q1s[i]
            grad = ratio(a - b, jnp.abs(a) + jnp.abs(b))
            cross = ratio(dew[i + 1] + dew[i], aew[i + 1] + aew[i])
            vy = ay[i, l] * grad - by[i, l] * cross
            gys[i] = jnp.maximum(vy, 0.0) * b + jnp.minimum(vy, 0.0) * a

        def finish(i):
            v, w = q1s[i + 1], wst[i + 1]
            grad = ratio(v - w, awe[i + 1])
            cross = ratio(swe[i + 2] - swe[i], awe[i + 2] + awe[i])
            vx = ax[i, l] * grad - bx[i, l] * cross
            gx = jnp.maximum(vx, 0.0) * w + jnp.minimum(vx, 0.0) * v
            fld[i + 2, l] = v - (east(gx, last_lane) - gx) - (gys[i + 1] - gys[i])

        for i in (0, 1, 2):
            face(i)
        for i in (0, 1):
            finish(i)
        for i in (6, 7, 8):
            face(i)
        for i in (6, 7):
            finish(i)

        @pl.when(number < PASSES - 1)
        def _():
            send_halo(1 - parity, l)

        for i in (3, 4, 5):
            face(i)
        for i in (2, 3, 4, 5):
            finish(i)
        return carry

    lax.fori_loop(0, PASSES * LEVS, level_pass, 0)

    def deliver(l, carry):
        for i in range(ROWS):
            for k in range(5):
                out_ref[l, pl.ds(8 * k + i, 8, stride=40), :] = fld[i + 2, l, 8 * k : 8 * k + 8, :]
        return carry

    lax.fori_loop(0, LEVS, deliver, 0)


def tiles_of(winds):
    return winds.reshape(LEVS, ROWS, NF, NB).transpose(0, 2, 1, 3).reshape(LEVS, NF * ROWS, NB)


def body(spectral, legendre, wave_table, courant_lon, courant_lat):
    table = jnp.pad(wave_table.reshape(128, SLOTS), ((0, 0), (0, 3)), constant_values=-1)
    table = table.reshape(1, 1024)
    parts = spectral.reshape(8, LEVS * SLOTS, K).transpose(1, 0, 2)
    vmem = pl.BlockSpec(memory_space=pltpu.VMEM)
    smem = pl.BlockSpec(memory_space=pltpu.SMEM)
    hbm = pl.BlockSpec(memory_space=pl.ANY)
    high, low = first_stage_tables()
    packing, two = pack_table(), second_stage_table()
    big = lambda rows: pltpu.VMEM((rows, LEVS, NF, NB), F32)
    small = lambda rows: pltpu.VMEM((rows, NF, NB), F32)
    dma = pltpu.SemaphoreType.DMA
    out = pl.pallas_call(
        whole_kernel,
        out_shape=jax.ShapeDtypeStruct((LEVS, NF * ROWS, NB), F32),
        in_specs=[smem, vmem] + [hbm] * 8,
        out_specs=vmem,
        scratch_shapes=[
            pltpu.VMEM(legendre.shape, BF16),
            pltpu.VMEM((LEVS, NF * ROWS, NB), F32),
            pltpu.VMEM((LEVS, NF * ROWS, NB), F32),
            pltpu.VMEM(packing.shape, BF16),
            pltpu.VMEM(high.shape, BF16),
            pltpu.VMEM(low.shape, BF16),
            pltpu.VMEM(two.shape, BF16),
            pltpu.VMEM((LEVS, SLOTS, 8, K), BF16),
            pltpu.VMEM((256, 128), F32),
            pltpu.VMEM((8, 256, 128), F32),
            pltpu.VMEM((WAVES, LEVS, 8, 128), BF16),
            pltpu.VMEM((128, 8, 128), BF16),
            pltpu.VMEM((640, 1024), BF16),
            pltpu.VMEM((5, 128, 128), F32),
            pltpu.VMEM((32, 2, NF, NB), F32),
            big(12), big(10), big(11), big(10), big(10), big(11), big(11),
            big(8), big(8), big(9), big(9),
            small(10), small(10), small(10), small(10), small(10), small(10), small(9),
            pltpu.VMEM((2, 2, LEVS, 2, NF, NB), BF16),
            pltpu.VMEM((2, 2, LEVS, 2, NF, NB), BF16),
            dma((8,)), dma((3, SLOTS)), dma((3, SLOTS)), dma, dma,
            dma((4,)), dma((4,)), dma((2, 2, LEVS)), dma((2, 2, LEVS)),
        ],
        compiler_params=pltpu.CompilerParams(collective_id=0, has_side_effects=True),
        name="whole",
    )(
        wave_table, table, parts, legendre, tiles_of(courant_lon), tiles_of(courant_lat),
        jnp.asarray(packing), jnp.asarray(high), jnp.asarray(low), jnp.asarray(two),
    )
    out = out.reshape(LEVS, NF, ROWS, NB).transpose(0, 2, 1, 3)
    return out.reshape(LEVS, ROWS, NLON)


def solution(mesh):
    placed = (
        P(None, "lev", "wave", None),
        P(("wave", "lev"), None, None),
        P(),
        P("lev", "wave", None),
        P("lev", "wave", None),
    )
    return jax.shard_map(
        body, mesh=mesh, in_specs=placed, out_specs=P("lev", "wave", None), check_vma=False
    )
```

```python
import math

import jax
import jax.numpy as jnp
import numpy as np
from jax import lax
from jax.experimental import pallas as pl
from jax.experimental.pallas import tpu as pltpu
from jax.sharding import PartitionSpec as P

M = 1280
NLON = 5120
K = 1281
PASSES = 4
WAVES = 32
LEVS = 4
SLOTS = 5
ROWS = 8
NF = 40
NB = 128
F32 = jnp.float32
BF16 = jnp.bfloat16
MESH = pl.DeviceIdType.MESH


def split_table(values):
    high = values.astype(np.float32).astype(BF16)
    low = (values - high.astype(np.float64)).astype(np.float32).astype(BF16)
    return high, low


def first_stage_tables():
    g = np.arange(5)[:, None, None, None]
    h = np.arange(2)[None, :, None, None]
    f8 = np.arange(8)[None, None, :, None]
    p1 = np.arange(16)[None, None, None, :]
    m = np.where(h == 0, 40 * p1 + 8 * g + f8, M - 1 - (40 * p1 + 8 * (4 - g) + f8))
    m = m.reshape(5, 256, 1)
    angle = 2.0 * math.pi / NLON * ((m * np.arange(NB)[None, None, :]) % NLON)
    weight = np.where(m == 0, 1.0, 2.0)
    return split_table(np.concatenate([weight * np.cos(angle), weight * np.sin(angle)], -1))


def second_stage_table():
    row = np.arange(NF)
    place = 5 * (row % 8) + row // 8
    angle = 2.0 * math.pi / NF * ((place[:, None] * np.arange(NF)[None, :]) % NF)
    high, low = split_table(np.concatenate([np.cos(angle), -np.sin(angle)], -1))
    return np.concatenate([high, low, high], -1)


def pack_table():
    t8 = np.arange(8)[:, None, None]
    lane = np.arange(128)[None, :, None]
    h, v, c, l = lane // 32, lane // 8 % 4, lane // 4 % 2, lane % 4
    goal = v * 128 + h * 64 + c * 32 + t8 * 4 + l
    hit = (goal == np.arange(512)[None, None, :]) & (lane < 64)
    return hit.astype(np.float32).astype(BF16)


def dot(a, b):
    return jnp.dot(a, b, preferred_element_type=F32)


def west(v, edge):
    r = pltpu.roll(v, 1, 1)
    before = jnp.concatenate([pltpu.roll(r[32:40], 1, 0), r[0:32]], 0)
    return jnp.where(edge, before, r)


def east(v, edge):
    r = pltpu.roll(v, 127, 1)
    after = jnp.concatenate([r[8:40], pltpu.roll(r[0:8], 7, 0)], 0)
    return jnp.where(edge, after, r)


def ratio(x, y):
    return x / jnp.maximum(y, 1.0)


def donor(u, low, high):
    return u * jnp.where(u > 0.0, low, high)


def whole_kernel(
    pairs_ref, spec_hbm, leg_hbm, lon_hbm, lat_hbm, pack_hbm, hi_hbm, lo_hbm, two_hbm,
    out_ref,
    spec_ref, leg_ref, lon_ref, lat_ref, pack_ref, hi_ref, lo_ref, two_ref,
    padded, sorted_ref, arrived, turned, lined, msgs, recv, column, choose,
    qt, ast, fld, cx, cy, cxp, cxm, cyp, cym, ax, bx, ay, by,
    q1s, abv, wst, swe, awe, dew, aew, gys, stage, halo, cstage, chalo,
    lsem, ssend, srecv, asend, arecv, csend, crecv, hsend, hrecv, round_sem,
):
    me = lax.axis_index("wave")
    lev = lax.axis_index("lev")
    rank = me * LEVS + lev
    up = lax.rem(me + 1, WAVES)
    down = lax.rem(me + WAVES - 1, WAVES)
    has_up = me < WAVES - 1
    has_down = me > 0

    at_z, at_x, at_y = me // 8, me // 4 % 2, me % 4
    z_peers = [lax.rem(me + 8 * n, WAVES) for n in (1, 2, 3)]
    y_peers = [me - at_y + lax.rem(at_y + n, 4) for n in (1, 2, 3)]
    x_peer = me + 4 - 8 * at_x
    barrier = pltpu.get_barrier_semaphore()

    def signal(sem, where):
        pl.semaphore_signal(sem, inc=1, device_id=where, device_id_type=MESH)

    for n in (1, 2, 3):
        signal(barrier, {"lev": lax.rem(lev + n, LEVS)})
    for peer in y_peers + z_peers + [x_peer]:
        signal(barrier, {"wave": peer})

    local = [
        pltpu.make_async_copy(a, b, lsem.at[n])
        for n, (a, b) in enumerate(
            [(spec_hbm, spec_ref), (lon_hbm, lon_ref), (lat_hbm, lat_ref), (leg_hbm, leg_ref),
             (pack_hbm, pack_ref), (hi_hbm, hi_ref), (lo_hbm, lo_ref), (two_hbm, two_ref)]
        )
    ]
    for copy in local:
        copy.start()

    def remote(src, dst, ssem, rsem, nb):
        return pltpu.make_async_remote_copy(
            src_ref=src, dst_ref=dst, send_sem=ssem, recv_sem=rsem,
            device_id={"wave": nb}, device_id_type=MESH,
        )

    goal = lax.broadcasted_iota(jnp.int32, (160, 256), 0)
    origin = lax.broadcasted_iota(jnp.int32, (160, 256), 1)
    moves = (goal // 8 == origin % 32) & (goal % 8 == origin // 32)
    padded[:, 16:32, :] = jnp.zeros((8, 16, K), BF16)
    local[0].wait()
    for n in range(8):
        padded[n, 0:20, :] = spec_ref[n]
    by_slot = dot(jnp.where(moves, 1.0, 0.0).astype(BF16), padded[...].reshape(256, K))
    sorted_ref[...] = by_slot.astype(BF16).reshape(20, 8, K)

    pl.semaphore_wait(barrier, 10)

    def spectral_copy(step, s):
        peer = lax.rem(lev + step, LEVS)
        return pltpu.make_async_remote_copy(
            src_ref=sorted_ref.at[peer * SLOTS + s],
            dst_ref=arrived.at[lev, s],
            send_sem=ssend.at[step - 1, s],
            recv_sem=srecv.at[step - 1, s],
            device_id={"lev": peer},
            device_id_type=MESH,
        )

    for s in range(SLOTS):
        for step in range(1, LEVS):
            spectral_copy(step, s).start()
    for peer in y_peers + z_peers:
        signal(round_sem.at[0], {"wave": peer})
    for s in range(SLOTS):
        arrived[lev, s] = sorted_ref[lev * SLOTS + s]

    local[1].wait()
    local[2].wait()

    def repack(l, carry):
        for i in range(ROWS):
            for k in range(5):
                cx[i + 1, l, 8 * k : 8 * k + 8, :] = lon_ref[l, pl.ds(8 * k + i, 8, stride=40), :]
                cy[i + 1, l, 8 * k : 8 * k + 8, :] = lat_ref[l, pl.ds(8 * k + i, 8, stride=40), :]
        cstage[0, l] = cx[8, l].astype(BF16)
        cstage[1, l] = cy[8, l].astype(BF16)
        cstage[2, l] = cx[1, l].astype(BF16)
        cstage[3, l] = cy[1, l].astype(BF16)
        cstage[4, l] = cy[2, l].astype(BF16)
        return carry

    lax.fori_loop(0, LEVS, repack, 0)

    pl.semaphore_wait(round_sem.at[0], 6)
    for n in (1, 2, 3):
        signal(round_sem.at[1], {"wave": lax.rem(me + 8 * n, WAVES)})
    for n in (0, 1, 2, 3):
        signal(round_sem.at[1], {"wave": lax.rem(x_peer + 8 * n, WAVES)})

    column[...] = jnp.full((1024, 128), -1, jnp.int32)

    def spread(n, carry):
        for s in range(SLOTS):
            column[pl.ds(n * 8 + s, 1), :] = jnp.full((1, 128), pairs_ref[n * SLOTS + s], jnp.int32)
        return carry

    lax.fori_loop(0, 128, spread, 0)
    place = lax.broadcasted_iota(jnp.int32, (1, 128), 1)
    for g in range(5):
        pair_of = 40 * (place % 16) + 8 * g + place // 16
        choose[:, g * 128 : (g + 1) * 128] = jnp.where(
            column[...] == pair_of, 1.0, 0.0
        ).astype(BF16)
    lined[...] = jnp.zeros_like(lined)

    lanes = lax.broadcasted_iota(jnp.int32, (NF, 128), 1)
    first_lane = lanes == 0
    last_lane = lanes == 127

    def split_x(r, l):
        u = cx[r, l]
        cxp[r, l] = jnp.maximum(u, 0.0)
        cxm[r, l] = jnp.minimum(u, 0.0)

    def split_y(r, l):
        v = cy[r, l]
        cyp[r, l] = jnp.maximum(v, 0.0)
        cym[r, l] = jnp.minimum(v, 0.0)

    def cross_x(i, l):
        pair = cy[i + 1, l] + cy[i + 2, l]
        bx[i, l] = (cx[i + 1, l] * 0.125) * (pair + west(pair, first_lane))

    def cross_y(i, l):
        pair = cx[i + 1, l] + cx[i, l]
        by[i, l] = (cy[i + 1, l] * 0.125) * (pair + east(pair, last_lane))

    def terms(l, carry):
        for i in range(ROWS):
            split_x(i + 1, l)
            split_y(i + 1, l)
            u = cx[i + 1, l]
            ax[i, l] = jnp.abs(u) - u * u
            v = cy[i + 1, l]
            ay[i, l] = jnp.abs(v) - v * v
            if i < ROWS - 1:
                cross_x(i, l)
            if i > 0:
                cross_y(i, l)
        return carry

    lax.fori_loop(0, LEVS, terms, 0)
    for copy in local[3:]:
        copy.wait()

    klane = lax.broadcasted_iota(jnp.int32, (1, K), 1)
    for s in range(SLOTS):
        for step in range(1, LEVS):
            spectral_copy(step, s).wait()
        low = klane < (M - pairs_ref[rank * SLOTS + s])
        spectra = arrived[:, s].reshape(32, K)
        zero = jnp.zeros_like(spectra)
        halves = jnp.concatenate(
            [jnp.where(low, spectra, zero), jnp.where(low, zero, spectra)], 0
        )
        total = dot(halves[:, : K - 1], leg_ref[s, : K - 1, :])
        last = spectra[:, K - 1 : K].astype(F32) * leg_ref[s, K - 1 : K, :].astype(F32)
        total = jnp.concatenate([total[:32], total[32:] + last], 0)
        rounded = total.astype(BF16).astype(F32)
        square = jnp.concatenate([rounded, jnp.zeros_like(rounded)], 0)
        turned[...] = square.T
        for t8 in range(8):
            lined[t8, pl.ds(s, WAVES, stride=8), :] = turned[pl.ds(t8, WAVES, stride=8), :]
    total = dot(lined[0].astype(BF16), pack_ref[0])
    for t8 in range(1, 8):
        total += dot(lined[t8].astype(BF16), pack_ref[t8])
    packed = total.astype(BF16)
    for v in range(LEVS):
        msgs[:, v] = packed[:, v * 128 : (v + 1) * 128].reshape(WAVES, 8, 128)

    pl.semaphore_wait(round_sem.at[1], 7)

    def scatter(step, carry):
        peer = lax.rem(rank + step, 128)
        pw, pv = peer // LEVS, peer % LEVS
        pltpu.make_async_remote_copy(
            src_ref=msgs.at[pw, pv], dst_ref=recv.at[rank], send_sem=asend, recv_sem=arecv,
            device_id={"wave": pw, "lev": pv}, device_id_type=MESH,
        ).start()
        return carry

    lax.fori_loop(1, 128, scatter, 0)
    recv[rank] = msgs[me, lev]
    courant = [
        remote(cstage.at[pl.ds(0, 2)], chalo.at[pl.ds(0, 2)], csend.at[0], crecv.at[0], up),
        remote(cstage.at[pl.ds(2, 3)], chalo.at[pl.ds(2, 3)], csend.at[1], crecv.at[1], down),
    ]
    for copy in courant:
        copy.start()

    blocks127 = recv.at[pl.ds(0, 127)]
    pltpu.make_async_copy(blocks127, blocks127, arecv).wait()
    pltpu.make_async_copy(blocks127, blocks127, asend).wait()

    ordered = lax.dot_general(
        recv[...].reshape(1024, 128), choose[...], (((0,), (0,)), ((), ())),
        preferred_element_type=F32,
    )
    for g in range(5):
        qt[g] = ordered[:, g * 128 : (g + 1) * 128]

    lane = lax.broadcasted_iota(jnp.int32, (8, 128), 1)
    sub = lax.broadcasted_iota(jnp.int32, (8, 128), 0)
    masks = (lane // 16 == sub, lane // 16 == 7 - sub)

    def first(g, carry):
        total = None
        for h in range(2):
            source = g if h == 0 else 4 - g
            rows = slice(h * 128, h * 128 + 128)
            th, tl = hi_ref[g, rows, :], lo_ref[g, rows, :]
            for c in range(2):
                blocks = []
                for x in range(32):
                    line = qt[source, pl.ds(h * 64 + c * 32 + x, 8, stride=0), :]
                    blocks.append(jnp.where(masks[h], line, 0.0))
                lhs = jnp.concatenate(blocks, 0).astype(BF16)
                for table in (th, tl):
                    if c == 1:
                        table = jnp.concatenate([-table[:, 128:], table[:, :128]], 1)
                    term = dot(lhs, table)
                    total = term if total is None else total + term
        total = total.reshape(32, 8, 256)
        at = pl.multiple_of(8 * g, 8)
        ast[:, 0, pl.ds(at, 8), :] = total[:, :, :128]
        ast[:, 1, pl.ds(at, 8), :] = total[:, :, 128:]
        return carry

    lax.fori_loop(0, 5, first, 0)

    def halo_copies(parity, l):
        return [
            remote(stage.at[parity, 1, l], halo.at[parity, 0, l],
                   hsend.at[parity, 0, l], hrecv.at[parity, 0, l], up),
            remote(stage.at[parity, 0, l], halo.at[parity, 1, l],
                   hsend.at[parity, 1, l], hrecv.at[parity, 1, l], down),
        ]

    def send_halo(parity, l):
        for i in range(2):
            stage[parity, 0, l, i] = fld[2 + i, l].astype(BF16)
            stage[parity, 1, l, i] = fld[8 + i, l].astype(BF16)
        for c in halo_copies(parity, l):
            c.start()

    def second(l, carry):
        for t in range(0, ROWS, 2):
            parts = []
            for u in (t, t + 1):
                both = ast[u * 4 + l].reshape(80, 128)
                high = both.astype(BF16)
                low = (both - high.astype(F32)).astype(BF16)
                parts.append(jnp.concatenate([high, high, low], 0))
            values = dot(two_ref[...], jnp.concatenate(parts, 1))
            fld[2 + t, l] = values[:, :128]
            fld[3 + t, l] = values[:, 128:]
        send_halo(0, l)
        return carry

    lax.fori_loop(0, LEVS, second, 0)

    zero = jnp.zeros((NF, 128), F32)

    def upwind(rows, l):
        flux = None
        for r in rows:
            q = fld[r + 2, l]
            if flux is None:
                flux = cyp[r + 1, l] * fld[r + 1, l] + cym[r + 1, l] * q
            above = cyp[r + 2, l] * q + cym[r + 2, l] * fld[r + 3, l]
            fx = cxp[r + 1, l] * west(q, first_lane) + cxm[r + 1, l] * q
            v = q - (east(fx, last_lane) - fx) - (above - flux)
            flux = above
            if r == -1:
                v = jnp.where(has_down, v, zero)
            if r == 8:
                v = jnp.where(has_up, v, zero)
            w = west(v, first_lane)
            e = east(v, last_lane)
            av = jnp.abs(v)
            aw = jnp.abs(w)
            q1s[l, r + 1] = v
            abv[l, r + 1] = av
            wst[l, r + 1] = w
            swe[l, r + 1] = v + w
            awe[l, r + 1] = av + aw
            dew[l, r + 1] = e - w
            aew[l, r + 1] = jnp.abs(e) + aw

    def face(i, l):
        a, b = q1s[l, i + 1], q1s[l, i]
        grad = ratio(a - b, abv[l, i + 1] + abv[l, i])
        cross = ratio(dew[l, i + 1] + dew[l, i], aew[l, i + 1] + aew[l, i])
        gys[l, i] = donor(ay[i, l] * grad - by[i, l] * cross, b, a)

    def finish(i, l):
        v, w = q1s[l, i + 1], wst[l, i + 1]
        grad = ratio(v - w, awe[l, i + 1])
        cross = ratio(swe[l, i + 2] - swe[l, i], awe[l, i + 2] + awe[l, i])
        gx = donor(ax[i, l] * grad - bx[i, l] * cross, w, v)
        fld[i + 2, l] = v - (east(gx, last_lane) - gx) - (gys[l, i + 1] - gys[l, i])

    def inner(l):
        upwind((1, 2, 3, 4, 5, 6), l)
        for i in (2, 3, 4, 5, 6):
            face(i, l)
        for i in (2, 3, 4, 5):
            finish(i, l)

    def outer(parity, l):
        for c in halo_copies(parity, l):
            c.wait()
        for i in range(2):
            fld[i, l] = jnp.where(has_down, halo[parity, 0, l, i].astype(F32), zero)
            fld[10 + i, l] = jnp.where(has_up, halo[parity, 1, l, i].astype(F32), zero)
        upwind((-1, 0), l)
        upwind((7, 8), l)
        for i in (0, 1, 7, 8):
            face(i, l)
        for i in (0, 1, 6, 7):
            finish(i, l)

    def first_inner(l, carry):
        inner(l)
        return carry

    lax.fori_loop(0, LEVS, first_inner, 0)
    for copy in courant:
        copy.wait()

    def first_outer(l, carry):
        cx[0, l] = jnp.where(has_down, chalo[0, l].astype(F32), zero)
        cy[0, l] = jnp.where(has_down, chalo[1, l].astype(F32), zero)
        cx[9, l] = jnp.where(has_up, chalo[2, l].astype(F32), zero)
        cy[9, l] = jnp.where(has_up, chalo[3, l].astype(F32), zero)
        cy[10, l] = jnp.where(has_up, chalo[4, l].astype(F32), zero)
        for r in (0, 9):
            split_x(r, l)
        for r in (0, 9, 10):
            split_y(r, l)
        v = cy[9, l]
        ay[8, l] = jnp.abs(v) - v * v
        cross_x(7, l)
        cross_y(0, l)
        cross_y(8, l)
        outer(0, l)
        send_halo(1, l)
        return carry

    lax.fori_loop(0, LEVS, first_outer, 0)

    def level_pass(step, carry):
        number = step // LEVS
        l = step % LEVS
        parity = number % 2
        inner(l)
        outer(parity, l)

        @pl.when(number < PASSES - 1)
        def _():
            send_halo(1 - parity, l)

        return carry

    lax.fori_loop(LEVS, PASSES * LEVS, level_pass, 0)

    def deliver(l, carry):
        for i in range(ROWS):
            for k in range(5):
                out_ref[l, pl.ds(8 * k + i, 8, stride=40), :] = fld[i + 2, l, 8 * k : 8 * k + 8, :]
        return carry

    lax.fori_loop(0, LEVS, deliver, 0)


def tiles_of(winds):
    return winds.reshape(LEVS, ROWS, NF, NB).transpose(0, 2, 1, 3).reshape(LEVS, NF * ROWS, NB)


def body(spectral, legendre, wave_table, courant_lon, courant_lat):
    parts = spectral.reshape(8, LEVS * SLOTS, K)
    vmem = pl.BlockSpec(memory_space=pltpu.VMEM)
    smem = pl.BlockSpec(memory_space=pltpu.SMEM)
    hbm = pl.BlockSpec(memory_space=pl.ANY)
    high, low = first_stage_tables()
    packing, two = pack_table(), second_stage_table()
    big = lambda rows: pltpu.VMEM((rows, LEVS, NF, NB), F32)
    small = lambda rows: pltpu.VMEM((LEVS, rows, NF, NB), F32)
    dma = pltpu.SemaphoreType.DMA
    out = pl.pallas_call(
        whole_kernel,
        out_shape=jax.ShapeDtypeStruct((LEVS, NF * ROWS, NB), F32),
        in_specs=[smem] + [hbm] * 8,
        out_specs=vmem,
        scratch_shapes=[
            pltpu.VMEM((8, LEVS * SLOTS, K), BF16),
            pltpu.VMEM(legendre.shape, BF16),
            pltpu.VMEM((LEVS, NF * ROWS, NB), F32),
            pltpu.VMEM((LEVS, NF * ROWS, NB), F32),
            pltpu.VMEM(packing.shape, BF16),
            pltpu.VMEM(high.shape, BF16),
            pltpu.VMEM(low.shape, BF16),
            pltpu.VMEM(two.shape, BF16),
            pltpu.VMEM((8, 32, K), BF16),
            pltpu.VMEM((LEVS * SLOTS, 8, K), BF16),
            pltpu.VMEM((LEVS, SLOTS, 8, K), BF16),
            pltpu.VMEM((256, 128), F32),
            pltpu.VMEM((8, 256, 128), F32),
            pltpu.VMEM((WAVES, LEVS, 8, 128), BF16),
            pltpu.VMEM((128, 8, 128), BF16),
            pltpu.VMEM((1024, 128), jnp.int32),
            pltpu.VMEM((1024, 640), BF16),
            pltpu.VMEM((5, 128, 128), F32),
            pltpu.VMEM((32, 2, NF, NB), F32),
            big(12), big(10), big(11), big(10), big(10), big(11), big(11),
            big(8), big(8), big(9), big(9),
            *[small(10)] * 7, small(9),
            pltpu.VMEM((2, 2, LEVS, 2, NF, NB), BF16),
            pltpu.VMEM((2, 2, LEVS, 2, NF, NB), BF16),
            pltpu.VMEM((5, LEVS, NF, NB), BF16),
            pltpu.VMEM((5, LEVS, NF, NB), BF16),
            dma((8,)), dma((3, SLOTS)), dma((3, SLOTS)), dma, dma,
            dma((2,)), dma((2,)), dma((2, 2, LEVS)), dma((2, 2, LEVS)),
            pltpu.SemaphoreType.REGULAR((2,)),
        ],
        compiler_params=pltpu.CompilerParams(collective_id=0, has_side_effects=True),
        name="whole",
    )(
        wave_table, parts, legendre, tiles_of(courant_lon), tiles_of(courant_lat),
        jnp.asarray(packing), jnp.asarray(high), jnp.asarray(low), jnp.asarray(two),
    )
    out = out.reshape(LEVS, NF, ROWS, NB).transpose(0, 2, 1, 3)
    return out.reshape(LEVS, ROWS, NLON)


def solution(mesh):
    placed = (
        P(None, "lev", "wave", None),
        P(("wave", "lev"), None, None),
        P(),
        P("lev", "wave", None),
        P("lev", "wave", None),
    )
    return jax.shard_map(
        body, mesh=mesh, in_specs=placed, out_specs=P("lev", "wave", None), check_vma=False
    )
```
